256 devices in a mesh: ep: 64 (over x, z, core), et: 4 (over y).
Axes of the slice: x: 4, y: 4, z: 8, core: 2. Of those that a mesh axis runs over, the one named last changes fastest.
Arguments:
- out_grad: bfloat16 [8192, 7168], P('ep', 'et'), may hold values from -0.1796875 to 0.1796875
- gate_weights: bfloat16 [8192, 8], P('ep'), may hold values from 0.049804688 to 1
- routes: int32 [8192, 8], P('ep'), may hold values from 0 to 63, as said below
- gate_pre: bfloat16 [64, 1152, 1024], P('ep', None, 'et'), may hold values from -6 to 6
- up_pre: bfloat16 [64, 1152, 1024], P('ep', None, 'et'), may hold values from -6 to 6
- down_weight: bfloat16 [64, 1024, 7168], P('ep', None, 'et'), may hold values from -0.1875 to 0.1875
Outputs:
- d_down_weight: bfloat16 [64, 1024, 7168], P('ep', None, 'et')
- d_gate: float32 [8192, 8], P('ep')
The draws below stay inside these ranges and needn't reach their ends.
Inputs may be any that keep to these rules, and one draw needn't show every extreme that they name: The experts in one row of routes differ. Among the rows of one source (one index of ep), at most 18 pairs name the same expert, and one expert is named by exactly 18 pairs of every source.
All inputs are finite; a program needn't handle non-finite values.
Results may differ from the reference program's by a relative error of at most 0.0057.
Values may be sent and summed in bfloat16 or wider, within the bound.
A program may use at most 64 MiB of HBM per device.

```python
import jax
import jax.numpy as jnp
from jax import lax

D = 7168
H = 1024
TOPK = 8
TOK_DEV = 128
EXPERTS = 64
CAP = 18
SLOTS = 1152
TOKENS = 8192
N_EP = 64


def draw_routes(key, part):
    mean_load = TOK_DEV * TOPK // EXPERTS
    spread = CAP - mean_load
    half = EXPERTS // 2
    hot = jax.random.randint(jax.random.fold_in(key, 1), (), 0, EXPERTS)
    positions = jnp.arange(TOK_DEV * TOPK, dtype=jnp.int32)

    def one_block(block_key):
        lift_key, order_key, token_key = jax.random.split(block_key, 3)
        lift = jax.random.randint(lift_key, (half,), 0, spread + 1)
        lift = lift.at[0].set(spread)
        loads = jnp.concatenate([mean_load + lift, mean_load - lift])
        starts = jnp.cumsum(loads) - loads
        order = jnp.concatenate([jnp.zeros((1,), jnp.int32), jax.random.permutation(order_key, EXPERTS - 1).astype(jnp.int32) + 1])
        labels = (hot + order) % EXPERTS
        which = jnp.sum((positions[:, None] >= starts[None, :]).astype(jnp.int32), axis=1) - 1
        expert_at = labels[which]
        token_order = jax.random.permutation(token_key, TOK_DEV).astype(jnp.int32)
        token = token_order[positions % TOK_DEV]
        column = positions // TOK_DEV
        return jnp.zeros((TOK_DEV, TOPK), jnp.int32).at[token, column].set(expert_at.astype(jnp.int32))
    block_keys = jax.random.split(jax.random.fold_in(key, 2), N_EP)
    return jax.vmap(one_block)(block_keys).reshape(TOKENS, TOPK).astype(jnp.int32)


def block_levels(own_key, extent, shards, least, largest):
    gain = 1.0
    for axis_at, shards_of in shards:
        steps = jax.random.uniform(jax.random.fold_in(jax.random.fold_in(own_key, 6), axis_at), (shards_of,), jnp.float32, least / len(shards), largest / len(shards))
        gain = gain * jnp.repeat(jnp.exp(steps), extent[axis_at] // shards_of).reshape((-1,) + (1,) * (len(extent) - 1 - axis_at))
    return gain


def gaussian(stream_key, dims, deviation, reach, cuts=(), held_as=jnp.bfloat16):
    level = block_levels(stream_key, dims, cuts, -0.22, 0.18) if cuts else 1.0
    result = jax.random.normal(stream_key, dims, jnp.float32) * deviation * level
    return jnp.minimum(jnp.maximum(result, -reach), reach).astype(held_as)


def setup_inputs(seed: int = 0) -> dict:
    arg_keys = jax.random.split(jax.random.key(seed), 7)
    return {
        "out_grad": gaussian(arg_keys[0], (TOKENS, D), 0.03, 0.1796875, ((0, 64), (1, 4))),
        "gate_weights": jnp.clip(0.049804688 + 0.9501953 * jax.random.uniform(arg_keys[1], (TOKENS, TOPK), jnp.float32) ** block_levels(arg_keys[1], (TOKENS, TOPK), ((0, 64),), -0.2, 0.2), 0.049804688, 1.0).astype(jnp.bfloat16),
        "routes": draw_routes(jax.random.fold_in(arg_keys[6], 71), 0),
        "gate_pre": gaussian(arg_keys[3], (EXPERTS, SLOTS, H), 1.0, 6.0, ((0, 64), (2, 4))),
        "up_pre": gaussian(arg_keys[4], (EXPERTS, SLOTS, H), 1.0, 6.0, ((0, 64), (2, 4))),
        "down_weight": gaussian(arg_keys[5], (EXPERTS, H, D), H ** -0.5, 0.1875, ((0, 64), (2, 4))),
    }


def reference(out_grad, gate_weights, routes, gate_pre, up_pre, down_weight):
    pairs = routes.reshape(N_EP, TOK_DEV * TOPK)
    onehot = (pairs[:, :, None] == jnp.arange(EXPERTS, dtype=jnp.int32)[None, None, :]).astype(jnp.int32)
    ranks = jnp.sum(jnp.cumsum(onehot, axis=1) * onehot, axis=2) - 1
    source = jnp.arange(N_EP, dtype=jnp.int32)[:, None]
    slot_of = (source * CAP + ranks).reshape(-1).astype(jnp.int32)
    flat_route = routes.reshape(-1)
    pair_ids = jnp.arange(TOKENS * TOPK, dtype=jnp.int32)
    flat_gates = gate_weights.reshape(-1)

    def one_expert(items):
        expert, gate_block, up_block, weight = items
        target = jnp.where(flat_route == expert, slot_of, SLOTS).astype(jnp.int32)
        slot_pair = jnp.zeros((SLOTS,), jnp.int32).at[target].set(pair_ids, mode="drop")
        filled = jnp.zeros((SLOTS,), jnp.bool_).at[target].set(True, mode="drop")
        rows = jnp.where(filled[:, None], out_grad[slot_pair // TOPK], 0.0).astype(jnp.bfloat16)
        gates = jnp.where(filled, flat_gates[slot_pair], 0.0).astype(jnp.bfloat16)
        hidden = (jax.nn.silu(gate_block.astype(jnp.float32)) * up_block.astype(jnp.float32)).astype(jnp.bfloat16)
        scaled = (gates.astype(jnp.float32)[:, None] * rows.astype(jnp.float32)).astype(jnp.bfloat16)
        grad_weight = jnp.dot(hidden.T, scaled, preferred_element_type=jnp.float32).astype(jnp.bfloat16)
        expert_out = jnp.dot(hidden, weight, preferred_element_type=jnp.float32)
        slot_grad = jnp.sum(rows.astype(jnp.float32) * expert_out, axis=1)
        return grad_weight, slot_grad

    experts_ids = jnp.arange(EXPERTS, dtype=jnp.int32)
    grads, slot_grads = lax.map(one_expert, (experts_ids, gate_pre, up_pre, down_weight))
    picked = (flat_route * SLOTS + slot_of).astype(jnp.int32)
    d_gate = slot_grads.reshape(-1)[picked].reshape(TOKENS, TOPK)
    return grads, d_gate
```

```python
import functools

import jax
import jax.numpy as jnp
from jax import lax
from jax.experimental import pallas as pl
from jax.experimental.pallas import tpu as pltpu
from jax.sharding import PartitionSpec as P

MESH = pl.DeviceIdType.MESH
F32 = jnp.float32
BF16 = jnp.bfloat16
NZ = 8
NC = 2
COLS = 256
TILE = 16


def zdelta(i):
    half = (i + 1) // 2
    return half if i % 2 else -half


def kernel(
    nx, nz, nc, ny, cap,
    routes_ref, gatew_ref, grad_hbm, gate_hbm, up_hbm, weight_hbm,
    dw_hbm, dg_ref,
    tok, meta, metaf, pick, xs, xm, rows, xmr, gate_v, up_v, raw, hid, hid_t, wts, eo, gates, acc,
    scaled, dw_v, small, small_t, rank_rel, sgp, sgy, sgt, sgx, zrow, zs, zin,
    in_sem, w_sem, out_sem, zsend, zrecv, xsend, xrecv, ysend, yrecv, tsend, trecv,
):
    nd = nx * nc
    experts = nx * nz * nc
    tokens, topk = routes_ref.shape
    blocks = tok.shape[0]
    per = nz * cap
    slots = nd * per
    hpart = gate_v.shape[1]
    ep, y = lax.axis_index("ep"), lax.axis_index("et")
    x, z, c = ep // (nz * nc), (ep // nc) % nz, ep % nc

    def device(dx, dz, dc, dy):
        xx, zz = lax.rem(x + (dx + nx), nx), lax.rem(z + (dz + nz), nz)
        cc, yy = lax.rem(c + dc, nc), lax.rem(y + (dy + ny), ny)
        return ((xx * nz + zz) * nc + cc, yy)

    def send(src, dst, ssem, rsem, to):
        return pltpu.make_async_remote_copy(
            src_ref=src, dst_ref=dst, send_sem=ssem, recv_sem=rsem, device_id=to, device_id_type=MESH
        )

    plane = [(d // nc, d % nc) for d in range(1, nd)]
    barrier = pltpu.get_barrier_semaphore()
    for i in range(1, nz):
        pl.semaphore_signal(barrier, inc=1, device_id=device(0, i, 0, 0), device_id_type=MESH)
    for dx, dc in plane:
        pl.semaphore_signal(barrier, inc=1, device_id=device(dx, 0, dc, 0), device_id_type=MESH)
    for dy in range(1, ny):
        pl.semaphore_signal(barrier, inc=1, device_id=device(0, 0, 0, dy), device_id_type=MESH)

    def tok_in(b):
        return pltpu.make_async_copy(
            grad_hbm.at[:, pl.ds(pl.multiple_of(b * COLS, COLS), COLS)], tok.at[b, 0], in_sem.at[b]
        )

    gate_in = pltpu.make_async_copy(gate_hbm.at[0], gate_v, in_sem.at[blocks])
    up_in = pltpu.make_async_copy(up_hbm.at[0], up_v, in_sem.at[blocks + 1])
    tok_in(0).start()
    gate_in.start()
    up_in.start()
    for b in range(1, blocks):
        tok_in(b).start()
    for b in range(blocks):
        for dy in range(ny):
            begin = pl.multiple_of(lax.rem(y + dy, ny) * hpart, hpart)
            pltpu.make_async_copy(
                weight_hbm.at[0, pl.ds(begin, hpart), b * COLS : (b + 1) * COLS],
                wts.at[b, dy * hpart : (dy + 1) * hpart],
                w_sem.at[b],
            ).start()

    small[...] = jnp.zeros_like(small)
    small[:, 0:topk] = routes_ref[...].astype(F32)
    small[:, 8 : 8 + topk] = gatew_ref[...].astype(F32)
    small_t[...] = small[...].T
    expert_id = lax.broadcasted_iota(jnp.int32, (experts, tokens), 0).astype(F32)
    member = jnp.zeros((experts, tokens), F32)
    gate_of = jnp.zeros((experts, tokens), F32)
    for k in range(topk):
        hit = small_t[k : k + 1, :] == expert_id
        member = jnp.where(hit, 1.0, member)
        gate_of = jnp.where(hit, small_t[8 + k : 9 + k, :], gate_of)
    before = (
        lax.broadcasted_iota(jnp.int32, (tokens, tokens), 0)
        < lax.broadcasted_iota(jnp.int32, (tokens, tokens), 1)
    )
    before = jnp.where(before, 1.0, 0.0).astype(BF16)
    rank = jnp.dot(member.astype(BF16), before, preferred_element_type=F32)
    rank = jnp.where(member > 0.0, rank, -100.0)
    meta[0, :, 0:tokens] = rank.astype(BF16)
    meta[0, :, tokens : 2 * tokens] = gate_of.astype(BF16)
    r_id = lax.broadcasted_iota(jnp.int32, (experts, experts), 0)
    e_id = lax.broadcasted_iota(jnp.int32, (experts, experts), 1)

    def rel_expert(r):
        i = r // nd
        half = (i + 1) // 2
        dz = jnp.where(i % 2 == 1, half, -half)
        d = r % nd
        return ((x + d // nc) % nx) * (nz * nc) + ((z + nz - dz) % nz) * nc + (c + d % nc) % nc

    order = jnp.where(rel_expert(r_id) == e_id, 1.0, 0.0).astype(BF16)
    rank_rel[...] = jnp.dot(order, rank.astype(BF16), preferred_element_type=F32)

    def zmsg(buf, sem, b, step, up):
        src = 0 if step == 1 else (2 * (step - 1) if up else 2 * (step - 1) - 1)
        extent = buf.shape[1]
        if step < nz // 2:
            dst = 2 * step if up else 2 * step - 1
            key = dst
            part = slice(0, extent)
        else:
            dst = nz - 1
            key = dst if up else 0
            part = slice(0, extent // 2) if up else slice(extent // 2, extent)
        return send(
            buf.at[src, part], buf.at[dst, part], zsend.at[sem], zrecv.at[sem, key],
            device(0, 1 if up else -1, 0, 0),
        )

    def zblock(b, step, up):
        return zmsg(tok.at[b], b, b, step, up)

    def zmeta(step, up):
        return zmsg(meta, blocks, 0, step, up)

    pl.semaphore_wait(barrier, (nz - 1) + (nd - 1) + (ny - 1))
    for up in (True, False):
        zmeta(1, up).start()
    tok_in(0).wait()
    for up in (True, False):
        zblock(0, 1, up).start()

    group = nz * nc * cap
    gate_in.wait()
    up_in.wait()
    row = lax.broadcasted_iota(jnp.int32, (group, group), 0)
    col = lax.broadcasted_iota(jnp.int32, (group, group), 1)
    g = (row * 3641) >> 16
    j = row - g * cap
    i = g % nz
    half = (i + 1) // 2
    zs_of = (z + nz + jnp.where(i % 2 == 1, half, -half)) % nz
    cs_of = (c + g // nz) % nc
    perm = jnp.where((zs_of * nc + cs_of) * cap + j == col, 1.0, 0.0).astype(BF16)
    for dx in range(nx):
        begin = pl.multiple_of(lax.rem(x + dx, nx) * group, 16)
        gv = gate_v[pl.ds(begin, group), :].astype(F32)
        uv = up_v[pl.ds(begin, group), :].astype(F32)
        raw[...] = (gv / (1.0 + jnp.exp(-gv)) * uv).astype(BF16)
        hid[dx * group : (dx + 1) * group, 0:hpart] = jnp.dot(
            perm, raw[...], preferred_element_type=F32
        ).astype(BF16)

    def ypart(dy, first):
        return hid.at[
            0 : slots // 2 if first else slots, dy * hpart : (dy + 1) * hpart
        ] if first else hid.at[slots // 2 : slots, dy * hpart : (dy + 1) * hpart]

    def ymsg(n):
        up, first, src, dst = (
            (True, True, 0, 3), (False, False, 0, 1), (True, False, 0, 3),
            (False, True, 0, 1), (True, True, 3, 2), (False, False, 1, 2),
        )[n]
        return send(
            ypart(src, first), ypart(dst, first), ysend.at[n], yrecv.at[n],
            device(0, 0, 0, 1 if up else -1),
        )

    if ny > 1:
        for n in range(4):
            ymsg(n).start()
    eye = jnp.where(
        lax.broadcasted_iota(jnp.int32, (hpart, hpart), 0)
        == lax.broadcasted_iota(jnp.int32, (hpart, hpart), 1), 1.0, 0.0,
    ).astype(BF16)

    def turn(dy):
        hid_t[dy * hpart : (dy + 1) * hpart, :] = lax.dot_general(
            eye, hid[:, dy * hpart : (dy + 1) * hpart], (((1,), (1,)), ((), ())),
            preferred_element_type=F32,
        ).astype(BF16)

    turn(0)
    acc[...] = jnp.zeros_like(acc)
    sgp[...] = jnp.zeros_like(sgp)
    zs[...] = jnp.zeros_like(zs)

    tiles = per // TILE

    def sources(n, size):
        return n * size // cap, (n * size + size - 1) // cap

    def build_pick():
        metaf[...] = meta[...].astype(F32)
        lane = lax.broadcasted_iota(jnp.int32, (TILE, tokens), 0).astype(F32)
        for d in range(nd):
            e = (lax.rem(x + d // nc, nx) * nz + z) * nc + lax.rem(c + d % nc, nc)
            for s in range(nz):
                line = metaf[s, pl.ds(e, 1), :]
                target = xmr.at[0] if d == 0 else xm.at[d]
                target[s : s + 1, :] = line[:, 0:tokens]
                target[nz + s : nz + s + 1, :] = line[:, tokens : 2 * tokens]
            block = xmr[0] if d == 0 else xm[d]
            for n in range(tiles):
                w = min(sources(n, TILE)[0], nz - 2)
                for side in range(2):
                    s = w + side
                    hit = block[s : s + 1, :] == lane + float(n * TILE - s * cap)
                    pick[n, d * TILE : (d + 1) * TILE, side * tokens : (side + 1) * tokens] = (
                        jnp.where(hit, 1.0, 0.0).astype(BF16)
                    )

    def back(d):
        return ((nx - d // nc) % nx) * nc + (nc - d % nc) % nc

    def xmeta(d):
        return send(
            xm.at[d], xmr.at[back(d)], xsend.at[blocks], xrecv.at[blocks],
            device(d // nc, 0, d % nc, 0),
        )

    def xblock(b, d):
        return send(
            xs.at[b, d], rows.at[b, back(d)], xsend.at[b], xrecv.at[b],
            device(d // nc, 0, d % nc, 0),
        )

    far_first = sorted(range(1, nd), key=lambda d: -min(d // nc, nx - d // nc))

    def select(b):
        for n in range(tiles):
            w = min(sources(n, TILE)[0], nz - 2)
            pair = tok[b, w : w + 2].reshape(2 * tokens, COLS)
            got = jnp.dot(pick[n], pair, preferred_element_type=F32).astype(BF16)
            span = slice(n * TILE, (n + 1) * TILE)
            rows[b, 0, span, :] = got[0:TILE]
            for d in range(1, nd):
                xs[b, d, span, :] = got[d * TILE : (d + 1) * TILE]
        for d in far_first:
            xblock(b, d).start()

    def all_of(buf, sem):
        pltpu.make_async_copy(buf, buf, sem).wait()

    def build_gates():
        sub = lax.broadcasted_iota(jnp.int32, (8, tokens), 0).astype(F32)

        def one(q, carry):
            for n in range(per // 8):
                lo, hi = sources(n, 8)
                value = jnp.zeros((8, tokens), F32)
                for s in range(lo, hi + 1):
                    hit = xmr[q, s : s + 1, :] == sub + float(n * 8 - s * cap)
                    value = jnp.where(hit, xmr[q, nz + s : nz + s + 1, :], value)
                total = jnp.sum(value, axis=1, keepdims=True)
                gates[pl.ds(pl.multiple_of(q * per + n * 8, 8), 8), :] = jnp.broadcast_to(
                    total, (8, tokens)
                )
            return carry

        lax.fori_loop(0, nd, one, 0)

    def dw_out(b, dy):
        begin = pl.multiple_of(lax.rem(y + dy, ny) * hpart, hpart)
        return pltpu.make_async_copy(
            dw_v.at[b, dy * hpart : (dy + 1) * hpart],
            dw_hbm.at[pl.ds(begin, hpart), pl.ds(pl.multiple_of(b * COLS, COLS), COLS)],
            out_sem.at[b],
        )

    def yback(dy):
        return send(
            sgp, sgy.at[(ny - dy) % ny], tsend.at[0], trecv.at[0], device(0, 0, 0, dy)
        )

    def xback(d):
        return send(
            sgt, sgx.at[back(d)], tsend.at[1], trecv.at[1], device(d // nc, 0, d % nc, 0)
        )

    def zback(i):
        return send(zs.at[i], zin.at[i], tsend.at[2], trecv.at[2], device(0, zdelta(i), 0, 0))

    def reduce_slots():
        ones = jnp.ones((8, tokens), F32)
        for q in range(nd):
            line = lax.dot_general(
                ones, acc[q * per : (q + 1) * per, :], (((1,), (1,)), ((), ())),
                preferred_element_type=F32, precision=lax.Precision.HIGHEST,
            )
            sgp[q : q + 1, 0:per] = line[0:1, :]
        for dy in range(1, ny):
            yback(dy).start()

    def finish():
        total = sgp[...]
        if ny > 1:
            all_of(sgy.at[1:ny], trecv.at[0])
            for dy in range(1, ny):
                total = total + sgy[dy]
        sgt[...] = total
        for d in far_first:
            xback(d).start()
        sgx[0] = total
        all_of(sgx.at[1:nd], trecv.at[1])
        for d in range(nd):
            q = back(d)
            zrow[d : d + 1, :] = sgx[d, q : q + 1, :]
        for s in range(nz - 1, -1, -1):
            part = zrow[:, s * cap : (s + 1) * cap]
            if s:
                zs[s, :, 0:cap] = part
                zback(s).start()
            else:
                zin[0, :, 0:cap] = part
        all_of(zin.at[1:nz], trecv.at[2])
        values = zin[...].reshape(nz * nd, 128)
        rr = rank_rel[...]
        value = jnp.zeros((experts, tokens), F32)
        for n in range(cap):
            value = jnp.where(rr == float(n), values[:, n : n + 1], value)
        ids = rel_expert(lax.broadcasted_iota(jnp.int32, (experts, tokens), 0)).astype(F32)
        for k in range(topk):
            hit = small_t[k : k + 1, :] == ids
            dg_ref[k : k + 1, :] = jnp.sum(jnp.where(hit, value, 0.0), axis=0, keepdims=True)

    def consume(b):
        all_of(wts.at[b], w_sem.at[b])
        eo[...] = jnp.dot(hid[...], wts[b], preferred_element_type=F32)
        all_of(rows.at[b, 1:nd], xrecv.at[b])

        def one(q, carry):
            span = pl.ds(pl.multiple_of(q * per, 8), per)
            r = rows[b, q].astype(F32)
            prod = r * eo[span, :]
            acc[span, :] += prod[:, 0:128] + prod[:, 128:256]
            gv = gates[span, :]
            scaled[pl.ds(pl.multiple_of(q * per, 16), per), 0:128] = (r[:, 0:128] * gv).astype(BF16)
            scaled[pl.ds(pl.multiple_of(q * per, 16), per), 128:256] = (r[:, 128:256] * gv).astype(BF16)
            return carry

        lax.fori_loop(0, nd, one, 0)

        @pl.when(b == blocks - 1)
        def _():
            reduce_slots()

        dw_v[b] = jnp.dot(hid_t[...], scaled[...], preferred_element_type=F32).astype(BF16)
        for dy in range(ny):
            dw_out(b, dy).start()

    depth = nz // 2

    def slot(t, carry):
        for step in range(depth, 0, -1):
            b = t - step

            def act(step=step, b=b):
                @pl.when(b == 0)
                def _():
                    for up in (True, False):
                        zmeta(step, up).wait_recv()
                        if step < depth:
                            zmeta(step + 1, up).start()

                for up in (True, False):
                    zblock(b, step, up).wait_recv()
                    if step < depth:
                        zblock(b, step + 1, up).start()

            pl.when((b >= 0) & (b < blocks))(act)

            if step == depth:
                @pl.when(b == 0)
                def _():
                    build_pick()
                    for d in far_first:
                        xmeta(d).start()

                @pl.when((b >= 0) & (b < blocks))
                def _(b=b):
                    select(b)

        @pl.when(t < blocks)
        def _():
            tok_in(t).wait()
            for up in (True, False):
                zblock(t, 1, up).start()

        if ny > 1:
            @pl.when(t == depth)
            def _():
                for n in (0, 1):
                    ymsg(n).wait_recv()
                for n in (4, 5):
                    ymsg(n).start()

        @pl.when(t == depth + 1)
        def _():
            all_of(xmr.at[1:nd], xrecv.at[blocks])
            build_gates()
            if ny > 1:
                for n in range(2, 6):
                    ymsg(n).wait_recv()
                for dy in range(1, ny):
                    turn(dy)

        b = t - depth - 1

        @pl.when(b >= 0)
        def _():
            consume(b)

        return carry

    lax.fori_loop(1, blocks + depth + 1, slot, 0)
    finish()

    for b in range(blocks):
        all_of(tok.at[b, 1:nz], zsend.at[b])
        all_of(xs.at[b, 1:nd], xsend.at[b])
        all_of(dw_v.at[b], out_sem.at[b])
    all_of(meta.at[1:nz], zsend.at[blocks])
    all_of(xm.at[1:nd], xsend.at[blocks])
    if ny > 1:
        for n in range(6):
            ymsg(n).wait_send()
        all_of(sgy.at[1:ny], tsend.at[0])
    all_of(sgx.at[1:nd], tsend.at[1])
    all_of(zs.at[1:nz], tsend.at[2])


def local(sizes, out_grad, gate_weights, routes, gate_pre, up_pre, down_weight):
    nx, nz, nc, ny = sizes
    tokens, topk = routes.shape
    width = out_grad.shape[1]
    blocks = width // COLS
    experts = nx * nz * nc
    nd = nx * nc
    slots, hpart = gate_pre.shape[1:]
    hidden = down_weight.shape[1]
    cap = slots // experts
    per = nz * cap
    anyspace = pl.BlockSpec(memory_space=pl.ANY)
    vmem = pl.BlockSpec(memory_space=pltpu.VMEM)
    dma = pltpu.SemaphoreType.DMA
    dw, dg = pl.pallas_call(
        functools.partial(kernel, nx, nz, nc, ny, cap),
        out_shape=(
            jax.ShapeDtypeStruct((hidden, width), BF16),
            jax.ShapeDtypeStruct((topk, tokens), F32),
        ),
        in_specs=[vmem, vmem, anyspace, anyspace, anyspace, anyspace],
        out_specs=(anyspace, vmem),
        scratch_shapes=[
            pltpu.VMEM((blocks, nz, tokens, COLS), BF16),
            pltpu.VMEM((nz, experts, 2 * tokens), BF16),
            pltpu.VMEM((nz, experts, 2 * tokens), F32),
            pltpu.VMEM((per // TILE, nd * TILE, 2 * tokens), BF16),
            pltpu.VMEM((blocks, nd, per, COLS), BF16),
            pltpu.VMEM((nd, 2 * nz, tokens), F32),
            pltpu.VMEM((blocks, nd, per, COLS), BF16),
            pltpu.VMEM((nd, 2 * nz, tokens), F32),
            pltpu.VMEM((slots, hpart), BF16),
            pltpu.VMEM((slots, hpart), BF16),
            pltpu.VMEM((nz * nc * cap, hpart), BF16),
            pltpu.VMEM((slots, hidden), BF16),
            pltpu.VMEM((hidden, slots), BF16),
            pltpu.VMEM((blocks, hidden, COLS), BF16),
            pltpu.VMEM((slots, COLS), F32),
            pltpu.VMEM((slots, 128), F32),
            pltpu.VMEM((slots, 128), F32),
            pltpu.VMEM((slots, COLS), BF16),
            pltpu.VMEM((blocks, hidden, COLS), BF16),
            pltpu.VMEM((tokens, 128), F32),
            pltpu.VMEM((128, tokens), F32),
            pltpu.VMEM((experts, tokens), F32),
            pltpu.VMEM((nd, 256), F32),
            pltpu.VMEM((ny, nd, 256), F32),
            pltpu.VMEM((nd, 256), F32),
            pltpu.VMEM((nd, nd, 256), F32),
            pltpu.VMEM((nd, 256), F32),
            pltpu.VMEM((nz, nd, 128), F32),
            pltpu.VMEM((nz, nd, 128), F32),
            dma((blocks + 2,)),
            dma((blocks,)),
            dma((blocks,)),
            dma((blocks + 1,)),
            dma((blocks + 1, nz)),
            dma((blocks + 1,)),
            dma((blocks + 1,)),
            dma((6,)),
            dma((6,)),
            dma((3,)),
            dma((3,)),
        ],
        compiler_params=pltpu.CompilerParams(collective_id=0, has_side_effects=True),
    )(routes, gate_weights, out_grad, gate_pre, up_pre, down_weight)
    return dw[None], dg.T


def solution(mesh):
    ny = mesh.shape["et"]
    nx = mesh.shape["ep"] // (NZ * NC)
    in_specs = (
        P("ep", "et"),
        P("ep", None),
        P("ep", None),
        P("ep", None, "et"),
        P("ep", None, "et"),
        P("ep", None, "et"),
    )
    out_specs = (P("ep", None, "et"), P("ep", None))
    return jax.shard_map(
        functools.partial(local, (nx, NZ, NC, ny)),
        mesh=mesh, in_specs=in_specs, out_specs=out_specs, check_vma=False,
    )
```

```python
import functools

import jax
import jax.numpy as jnp
from jax import lax
from jax.experimental import pallas as pl
from jax.experimental.pallas import tpu as pltpu
from jax.sharding import PartitionSpec as P

MESH = pl.DeviceIdType.MESH
F32 = jnp.float32
BF16 = jnp.bfloat16
NZ = 8
NC = 2
COLS = 256
LAG = 2
TILE = 16


def zdelta(i):
    half = (i + 1) // 2
    return half if i % 2 else -half


def kernel(
    nx, nz, nc, ny, cap,
    routes_hbm, gatew_hbm, grad_hbm, gate_hbm, up_hbm, weight_hbm,
    dw_ref, dg_ref,
    routes_v, gatew_v, tok, meta, ahead, pick, pick_more, xs, xm, rows, xmr, gate_v, up_v, raw, hid, hid_t, wts, eo, gates, acc,
    scaled, rank_rel, sgp, sgy, sgt, sgx, zrow, zs, zin,
    in_sem, w_sem, zsend, zrecv, xsend, xrecv, ysend, yrecv, tsend, trecv,
):
    nd = nx * nc
    experts = nx * nz * nc
    topk, tokens = routes_hbm.shape
    extra = cap - TILE
    blocks = tok.shape[0]
    per = nz * cap
    slots = nd * per
    hpart = gate_v.shape[1]
    ep, y = lax.axis_index("ep"), lax.axis_index("et")
    x, z, c = ep // (nz * nc), (ep // nc) % nz, ep % nc

    def device(dx, dz, dc, dy):
        xx, zz = lax.rem(x + (dx + nx), nx), lax.rem(z + (dz + nz), nz)
        cc, yy = lax.rem(c + dc, nc), lax.rem(y + (dy + ny), ny)
        return ((xx * nz + zz) * nc + cc, yy)

    def send(src, dst, ssem, rsem, to):
        return pltpu.make_async_remote_copy(
            src_ref=src, dst_ref=dst, send_sem=ssem, recv_sem=rsem, device_id=to, device_id_type=MESH
        )

    plane = [(d // nc, d % nc) for d in range(1, nd)]
    barrier = pltpu.get_barrier_semaphore()
    for dz in (1, nz - 1):
        pl.semaphore_signal(barrier, inc=1, device_id=device(0, dz, 0, 0), device_id_type=MESH)
    for dx, dc in plane:
        pl.semaphore_signal(barrier, inc=1, device_id=device(dx, 0, dc, 0), device_id_type=MESH)
    for dy in range(1, ny):
        pl.semaphore_signal(barrier, inc=1, device_id=device(0, 0, 0, dy), device_id_type=MESH)

    def tok_in(b):
        return pltpu.make_async_copy(
            grad_hbm.at[:, pl.ds(pl.multiple_of(b * COLS, COLS), COLS)], tok.at[b, 0], in_sem.at[b]
        )

    gate_in = pltpu.make_async_copy(gate_hbm.at[0], gate_v, in_sem.at[blocks])
    up_in = pltpu.make_async_copy(up_hbm.at[0], up_v, in_sem.at[blocks + 1])
    routes_in = pltpu.make_async_copy(routes_hbm, routes_v, in_sem.at[blocks + 2])
    gatew_in = pltpu.make_async_copy(gatew_hbm, gatew_v, in_sem.at[blocks + 3])
    routes_in.start()
    gatew_in.start()
    tok_in(0).start()
    gate_in.start()
    up_in.start()
    for b in range(1, blocks):
        tok_in(b).start()
    for b in range(blocks):
        for dy in range(ny):
            begin = pl.multiple_of(lax.rem(y + dy, ny) * hpart, hpart)
            pltpu.make_async_copy(
                weight_hbm.at[0, pl.ds(begin, hpart), b * COLS : (b + 1) * COLS],
                wts.at[b, dy * hpart : (dy + 1) * hpart],
                w_sem.at[b],
            ).start()

    earlier = (
        lax.broadcasted_iota(jnp.int32, (tokens, tokens), 0)
        < lax.broadcasted_iota(jnp.int32, (tokens, tokens), 1)
    )
    ahead[...] = jnp.where(earlier, 1.0, 0.0).astype(BF16)
    routes_in.wait()
    gatew_in.wait()
    meta[0, 0:topk, :] = routes_v[...].astype(F32)
    meta[0, topk : 2 * topk, :] = gatew_v[...].astype(F32)

    def ranks(s, ids):
        member = jnp.zeros(ids.shape, F32)
        gate_of = jnp.zeros(ids.shape, F32)
        for k in range(topk):
            hit = meta[s, k : k + 1, :] == ids
            member = jnp.where(hit, 1.0, member)
            gate_of = jnp.where(hit, meta[s, topk + k : topk + k + 1, :], gate_of)
        rank = jnp.dot(member.astype(BF16), ahead[...], preferred_element_type=F32)
        return jnp.where(member > 0.0, rank, -100.0), gate_of

    def rel_expert(r):
        i = r // nd
        half = (i + 1) // 2
        dz = jnp.where(i % 2 == 1, half, -half)
        d = r % nd
        return ((x + d // nc) % nx) * (nz * nc) + ((z + nz - dz) % nz) * nc + (c + d % nc) % nc

    def zmsg(buf, sem, b, step, up):
        src = 0 if step == 1 else (2 * (step - 1) if up else 2 * (step - 1) - 1)
        extent = buf.shape[1]
        if step < nz // 2:
            dst = 2 * step if up else 2 * step - 1
            key = dst
            part = slice(0, extent)
        else:
            dst = nz - 1
            key = dst if up else 0
            part = slice(0, extent // 2) if up else slice(extent // 2, extent)
        return send(
            buf.at[src, part], buf.at[dst, part], zsend.at[sem], zrecv.at[sem, key],
            device(0, 1 if up else -1, 0, 0),
        )

    def zblock(b, step, up):
        return zmsg(tok.at[b], b, b, step, up)

    def zmeta(step, up):
        return zmsg(meta, blocks, 0, step, up)

    def build_pick(which):
        lane = lax.broadcasted_iota(jnp.int32, (TILE, tokens), 0)
        d_id = lax.broadcasted_iota(jnp.int32, (nd, tokens), 0)
        ids = (((x + d_id // nc) % nx) * nz + z) * nc + (c + d_id % nc) % nc
        for s in which:
            rank_of, gate_of = ranks(s, ids.astype(F32))
            for d in range(nd):
                target = xmr.at[0] if d == 0 else xm.at[d]
                line = rank_of[d : d + 1, :]
                target[s : s + 1, :] = line
                target[nz + s : nz + s + 1, :] = gate_of[d : d + 1, :]
                span = slice(d * TILE, (d + 1) * TILE)
                pick[s, span, :] = jnp.where(line == lane.astype(F32), 1.0, 0.0).astype(BF16)
                more = jnp.where(lane // extra == s, TILE + lane % extra, -1).astype(F32)
                pick_more[span, s * tokens : (s + 1) * tokens] = jnp.where(
                    line == more, 1.0, 0.0
                ).astype(BF16)

    def back(d):
        return ((nx - d // nc) % nx) * nc + (nc - d % nc) % nc

    far_first = sorted(range(1, nd), key=lambda d: -min(d // nc, nx - d // nc))

    def xmeta(d):
        return send(
            xm.at[d], xmr.at[back(d)], xsend.at[blocks], xrecv.at[blocks],
            device(d // nc, 0, d % nc, 0),
        )

    def place(b, n, got):
        got = got.astype(BF16)
        rows[b, 0, n * TILE : (n + 1) * TILE, :] = got[0:TILE]
        for d in range(1, nd):
            xs[b, d, n * TILE : (n + 1) * TILE, :] = got[d * TILE : (d + 1) * TILE]

    def select(b, which):
        for s in which:
            place(b, s, jnp.dot(pick[s], tok[b, s], preferred_element_type=F32))
        last = which[-1]
        if last == nz - 1:
            every = tok[b].reshape(nz * tokens, COLS)
            place(b, nz, jnp.dot(pick_more[...], every, preferred_element_type=F32))
            last = nz
        span = slice(which[0] * TILE, (last + 1) * TILE)
        for d in far_first:
            send(
                xs.at[b, d, span], rows.at[b, back(d), span], xsend.at[b], xrecv.at[b],
                device(d // nc, 0, d % nc, 0),
            ).start()

    pl.semaphore_wait(barrier, 2 + (nd - 1) + (ny - 1))
    for up in (True, False):
        zmeta(1, up).start()
    tok_in(0).wait()
    for up in (True, False):
        zblock(0, 1, up).start()
    build_pick((0,))
    select(0, (0,))

    group = nz * nc * cap
    gate_in.wait()
    up_in.wait()
    row = lax.broadcasted_iota(jnp.int32, (group, group), 0)
    col = lax.broadcasted_iota(jnp.int32, (group, group), 1)
    dc = jnp.zeros_like(row)
    for n in range(1, nc):
        dc = jnp.where(row >= n * per, n, dc)
    inner = row - dc * per
    i = jnp.where(inner < nz * TILE, inner // TILE, (inner - nz * TILE) // extra)
    j = jnp.where(inner < nz * TILE, inner % TILE, TILE + inner % extra)
    half = (i + 1) // 2
    zs_of = (z + nz + jnp.where(i % 2 == 1, half, -half)) % nz
    cs_of = (c + dc) % nc
    perm = jnp.where((zs_of * nc + cs_of) * cap + j == col, 1.0, 0.0).astype(BF16)
    for dx in range(nx):
        begin = pl.multiple_of(lax.rem(x + dx, nx) * group, 16)
        gv = gate_v[pl.ds(begin, group), :].astype(F32)
        uv = up_v[pl.ds(begin, group), :].astype(F32)
        raw[...] = (gv / (1.0 + jnp.exp(-gv)) * uv).astype(BF16)
        hid[dx * group : (dx + 1) * group, 0:hpart] = jnp.dot(
            perm, raw[...], preferred_element_type=F32
        ).astype(BF16)

    def ypart(dy, first):
        return hid.at[
            0 : slots // 2 if first else slots, dy * hpart : (dy + 1) * hpart
        ] if first else hid.at[slots // 2 : slots, dy * hpart : (dy + 1) * hpart]

    def ymsg(n):
        up, first, src, dst = (
            (True, True, 0, 3), (False, False, 0, 1), (True, False, 0, 3),
            (False, True, 0, 1), (True, True, 3, 2), (False, False, 1, 2),
        )[n]
        return send(
            ypart(src, first), ypart(dst, first), ysend.at[n], yrecv.at[n],
            device(0, 0, 0, 1 if up else -1),
        )

    if ny > 1:
        for n in range(4):
            ymsg(n).start()
    eye = jnp.where(
        lax.broadcasted_iota(jnp.int32, (hpart, hpart), 0)
        == lax.broadcasted_iota(jnp.int32, (hpart, hpart), 1), 1.0, 0.0,
    ).astype(BF16)

    def turn(dy):
        hid_t[dy * hpart : (dy + 1) * hpart, :] = lax.dot_general(
            eye, hid[:, dy * hpart : (dy + 1) * hpart], (((1,), (1,)), ((), ())),
            preferred_element_type=F32,
        ).astype(BF16)

    turn(0)
    rel_ids = rel_expert(lax.broadcasted_iota(jnp.int32, (experts, tokens), 0)).astype(F32)
    rank_rel[...] = ranks(0, rel_ids)[0]
    for b in range(1, blocks):
        tok_in(b).wait()
    acc[...] = jnp.zeros_like(acc)
    sgp[...] = jnp.zeros_like(sgp)
    zs[...] = jnp.zeros_like(zs)

    def all_of(buf, sem):
        pltpu.make_async_copy(buf, buf, sem).wait()

    def build_gates():
        sub = lax.broadcasted_iota(jnp.int32, (8, tokens), 0)

        def one(q, carry):
            for n in range(per // 8):
                value = jnp.zeros((8, tokens), F32)
                if n * 8 < nz * TILE:
                    wanted = [(n * 8 // TILE, sub + n * 8 % TILE)]
                else:
                    first = n * 8 - nz * TILE
                    wanted = [
                        (s, jnp.where((sub + first) // extra == s, TILE + (sub + first) % extra, -1))
                        for s in range(first // extra, (first + 7) // extra + 1)
                    ]
                for s, rank_at in wanted:
                    hit = xmr[q, s : s + 1, :] == rank_at.astype(F32)
                    value = jnp.where(hit, xmr[q, nz + s : nz + s + 1, :], value)
                total = jnp.sum(value, axis=1, keepdims=True)
                gates[pl.ds(pl.multiple_of(q * per + n * 8, 8), 8), :] = jnp.broadcast_to(
                    total, (8, tokens)
                )
            return carry

        lax.fori_loop(0, nd, one, 0)

    def yback(dy):
        return send(
            sgp, sgy.at[(ny - dy) % ny], tsend.at[0], trecv.at[0], device(0, 0, 0, dy)
        )

    def xback(d):
        return send(
            sgt.at[d], sgx.at[back(d)], tsend.at[1], trecv.at[1], device(d // nc, 0, d % nc, 0)
        )

    def zback(i):
        return send(zs.at[i], zin.at[i], tsend.at[2], trecv.at[2], device(0, zdelta(i), 0, 0))

    def reduce_slots():
        ones = jnp.ones((8, tokens), F32)
        for q in range(nd):
            line = lax.dot_general(
                ones, acc[q * per : (q + 1) * per, :], (((1,), (1,)), ((), ())),
                preferred_element_type=F32, precision=lax.Precision.HIGHEST,
            )
            sgp[q : q + 1, 0:per] = line[0:1, :]
        for dy in range(1, ny):
            yback(dy).start()

    def finish():
        total = sgp[...]
        if ny > 1:
            all_of(sgy.at[1:ny], trecv.at[0])
            for dy in range(1, ny):
                total = total + sgy[dy]
        for d in far_first:
            sgt[d] = total[d : d + 1, :]
            xback(d).start()
        sgx[0] = total[0:1, :]
        all_of(sgx.at[1:nd], trecv.at[1])
        for d in range(nd):
            zrow[d : d + 1, :] = sgx[d]
        for s in range(nz - 1, -1, -1):
            target = zs.at[s] if s else zin.at[0]
            target[:, 0:TILE] = zrow[:, s * TILE : (s + 1) * TILE]
            more = nz * TILE + s * extra
            target[:, TILE:cap] = zrow[:, more : more + extra]
            if s:
                zback(s).start()
        all_of(zin.at[1:nz], trecv.at[2])
        values = zin[...].reshape(nz * nd, 128)
        rr = rank_rel[...]
        value = jnp.zeros((experts, tokens), F32)
        for n in range(cap):
            value = jnp.where(rr == float(n), values[:, n : n + 1], value)
        for k in range(topk):
            hit = meta[0, k : k + 1, :] == rel_ids
            dg_ref[k : k + 1, :] = jnp.sum(jnp.where(hit, value, 0.0), axis=0, keepdims=True)

    def consume(b):
        all_of(wts.at[b], w_sem.at[b])
        eo[...] = jnp.dot(hid[...], wts[b], preferred_element_type=F32)
        all_of(rows.at[b, 1:nd], xrecv.at[b])

        def one(q, carry):
            span = pl.ds(pl.multiple_of(q * per, 8), per)
            r = rows[b, q].astype(F32)
            prod = r * eo[span, :]
            acc[span, :] += prod[:, 0:128] + prod[:, 128:256]
            gv = gates[span, :]
            scaled[pl.ds(pl.multiple_of(q * per, 16), per), 0:128] = (r[:, 0:128] * gv).astype(BF16)
            scaled[pl.ds(pl.multiple_of(q * per, 16), per), 128:256] = (r[:, 128:256] * gv).astype(BF16)
            return carry

        lax.fori_loop(0, nd, one, 0)

        @pl.when(b == blocks - 1)
        def _():
            reduce_slots()

        span = pl.ds(pl.multiple_of(b * COLS, COLS), COLS)
        for dy in range(ny):
            begin = pl.multiple_of(lax.rem(y + dy, ny) * hpart, hpart)
            dw_ref[pl.ds(begin, hpart), span] = jnp.dot(
                hid_t[dy * hpart : (dy + 1) * hpart, :], scaled[...], preferred_element_type=F32
            ).astype(BF16)

    depth = nz // 2

    def slot(t, carry):
        for step in range(depth, 0, -1):
            b = t - step

            def act(step=step, b=b):
                @pl.when(b == 0)
                def _():
                    for up in (True, False):
                        zmeta(step, up).wait_recv()
                        if step < depth:
                            zmeta(step + 1, up).start()

                for up in (True, False):
                    zblock(b, step, up).wait_recv()
                    if step < depth:
                        zblock(b, step + 1, up).start()

                fresh = (2 * step - 1, 2 * step) if step < depth else (nz - 1,)

                @pl.when(b == 0)
                def _():
                    build_pick(fresh)
                    if step == depth:
                        for d in far_first:
                            xmeta(d).start()

                select(b, fresh)

            pl.when((b >= 0) & (b < blocks))(act)


        @pl.when(t < blocks)
        def _():
            for up in (True, False):
                zblock(t, 1, up).start()

        for own in (2 * t - 1, 2 * t):
            @pl.when(own < blocks)
            def _(own=own):
                select(own, (0,))

        if ny > 1:
            @pl.when(t == depth)
            def _():
                for n in (0, 1):
                    ymsg(n).wait_recv()
                for n in (4, 5):
                    ymsg(n).start()

        @pl.when(t == depth + LAG)
        def _():
            all_of(xmr.at[1:nd], xrecv.at[blocks])
            build_gates()
            if ny > 1:
                for n in range(2, 6):
                    ymsg(n).wait_recv()
                for dy in range(1, ny):
                    turn(dy)

        b = t - depth - LAG

        @pl.when(b >= 0)
        def _():
            consume(b)

        return carry

    lax.fori_loop(1, blocks + depth + LAG, slot, 0)
    finish()

    for b in range(blocks):
        all_of(tok.at[b, 1:nz], zsend.at[b])
        all_of(xs.at[b, 1:nd], xsend.at[b])
    all_of(meta.at[1:nz], zsend.at[blocks])
    all_of(xm.at[1:nd], xsend.at[blocks])
    if ny > 1:
        for n in range(6):
            ymsg(n).wait_send()
        all_of(sgy.at[1:ny], tsend.at[0])
    all_of(sgx.at[1:nd], tsend.at[1])
    all_of(zs.at[1:nz], tsend.at[2])


def local(sizes, out_grad, gate_weights, routes, gate_pre, up_pre, down_weight):
    nx, nz, nc, ny = sizes
    routes, gate_weights = routes.T, gate_weights.T
    topk, tokens = routes.shape
    width = out_grad.shape[1]
    blocks = width // COLS
    experts = nx * nz * nc
    nd = nx * nc
    slots, hpart = gate_pre.shape[1:]
    hidden = down_weight.shape[1]
    cap = slots // experts
    per = nz * cap
    hbm = pl.BlockSpec(memory_space=pltpu.HBM)
    vmem = pl.BlockSpec(memory_space=pltpu.VMEM)
    dma = pltpu.SemaphoreType.DMA
    dw, dg = pl.pallas_call(
        functools.partial(kernel, nx, nz, nc, ny, cap),
        out_shape=(
            jax.ShapeDtypeStruct((hidden, width), BF16),
            jax.ShapeDtypeStruct((topk, tokens), F32),
        ),
        in_specs=[hbm] * 6,
        out_specs=(vmem, vmem),
        scratch_shapes=[
            pltpu.VMEM((topk, tokens), jnp.int32),
            pltpu.VMEM((topk, tokens), BF16),
            pltpu.VMEM((blocks, nz, tokens, COLS), BF16),
            pltpu.VMEM((nz, 2 * topk, tokens), F32),
            pltpu.VMEM((tokens, tokens), BF16),
            pltpu.VMEM((nz, nd * TILE, tokens), BF16),
            pltpu.VMEM((nd * TILE, nz * tokens), BF16),
            pltpu.VMEM((blocks, nd, per, COLS), BF16),
            pltpu.VMEM((nd, 2 * nz, tokens), F32),
            pltpu.VMEM((blocks, nd, per, COLS), BF16),
            pltpu.VMEM((nd, 2 * nz, tokens), F32),
            pltpu.VMEM((slots, hpart), BF16),
            pltpu.VMEM((slots, hpart), BF16),
            pltpu.VMEM((nz * nc * cap, hpart), BF16),
            pltpu.VMEM((slots, hidden), BF16),
            pltpu.VMEM((hidden, slots), BF16),
            pltpu.VMEM((blocks, hidden, COLS), BF16),
            pltpu.VMEM((slots, COLS), F32),
            pltpu.VMEM((slots, 128), F32),
            pltpu.VMEM((slots, 128), F32),
            pltpu.VMEM((slots, COLS), BF16),
            pltpu.VMEM((experts, tokens), F32),
            pltpu.VMEM((nd, 256), F32),
            pltpu.VMEM((ny, nd, 256), F32),
            pltpu.VMEM((nd, 1, 256), F32),
            pltpu.VMEM((nd, 1, 256), F32),
            pltpu.VMEM((nd, 256), F32),
            pltpu.VMEM((nz, nd, 128), F32),
            pltpu.VMEM((nz, nd, 128), F32),
            dma((blocks + 4,)),
            dma((blocks,)),
            dma((blocks + 1,)),
            dma((blocks + 1, nz)),
            dma((blocks + 1,)),
            dma((blocks + 1,)),
            dma((6,)),
            dma((6,)),
            dma((3,)),
            dma((3,)),
        ],
        compiler_params=pltpu.CompilerParams(collective_id=0, has_side_effects=True, vmem_limit_bytes=44 * 2**20),
    )(
        *(
            pltpu.with_memory_space_constraint(v, pltpu.HBM)
            for v in (routes, gate_weights, out_grad, gate_pre, up_pre, down_weight)
        )
    )
    return dw[None], dg.T


def solution(mesh):
    ny = mesh.shape["et"]
    nx = mesh.shape["ep"] // (NZ * NC)
    in_specs = (
        P("ep", "et"),
        P("ep", None),
        P("ep", None),
        P("ep", None, "et"),
        P("ep", None, "et"),
        P("ep", None, "et"),
    )
    out_specs = (P("ep", None, "et"), P("ep", None))
    return jax.shard_map(
        functools.partial(local, (nx, NZ, NC, ny)),
        mesh=mesh, in_specs=in_specs, out_specs=out_specs, check_vma=False,
    )
```

```python
import functools

import jax
import jax.numpy as jnp
from jax import lax
from jax.experimental import pallas as pl
from jax.experimental.pallas import tpu as pltpu
from jax.sharding import PartitionSpec as P

MESH = pl.DeviceIdType.MESH
F32 = jnp.float32
BF16 = jnp.bfloat16
NZ = 8
NC = 2
COLS = 256
LAG = 2
LATE = 3
TILE = 16


def zdelta(i):
    half = (i + 1) // 2
    return half if i % 2 else -half


def kernel(
    nx, nz, nc, ny, cap,
    routes_hbm, gatew_hbm, grad_hbm, gate_hbm, up_hbm, weight_hbm,
    dw_ref, dg_ref,
    routes_v, gatew_v, tok, meta, ahead, pick, pick_more, xs, xm, rows, xmr, gate_v, up_v, raw, hid, hid_t, wts, eo, gates, acc,
    scaled, rank_rel, sgp, sgy, sgt, sgx, zrow, sgp_near, sgy_near, sgt_near, sgx_near, zrow_near, zs, zin,
    in_sem, w_sem, zsend, zrecv, xsend, xrecv, ysend, yrecv, tsend, trecv,
):
    nd = nx * nc
    experts = nx * nz * nc
    topk, tokens = routes_hbm.shape
    extra = cap - TILE
    blocks = tok.shape[0]
    per = nz * cap
    slots = nd * per
    hpart = gate_v.shape[1]
    ep, y = lax.axis_index("ep"), lax.axis_index("et")
    x, z, c = ep // (nz * nc), (ep // nc) % nz, ep % nc

    def device(dx, dz, dc, dy):
        xx, zz = lax.rem(x + (dx + nx), nx), lax.rem(z + (dz + nz), nz)
        cc, yy = lax.rem(c + dc, nc), lax.rem(y + (dy + ny), ny)
        return ((xx * nz + zz) * nc + cc, yy)

    def send(src, dst, ssem, rsem, to):
        return pltpu.make_async_remote_copy(
            src_ref=src, dst_ref=dst, send_sem=ssem, recv_sem=rsem, device_id=to, device_id_type=MESH
        )

    plane = [(d // nc, d % nc) for d in range(1, nd)]
    barrier = pltpu.get_barrier_semaphore()
    for dz in (1, nz - 1):
        pl.semaphore_signal(barrier, inc=1, device_id=device(0, dz, 0, 0), device_id_type=MESH)
    for dx, dc in plane:
        pl.semaphore_signal(barrier, inc=1, device_id=device(dx, 0, dc, 0), device_id_type=MESH)
    for dy in range(1, ny):
        pl.semaphore_signal(barrier, inc=1, device_id=device(0, 0, 0, dy), device_id_type=MESH)

    def tok_in(b):
        return pltpu.make_async_copy(
            grad_hbm.at[:, pl.ds(pl.multiple_of(b * COLS, COLS), COLS)], tok.at[b, 0], in_sem.at[b]
        )

    gate_in = pltpu.make_async_copy(gate_hbm.at[0], gate_v, in_sem.at[blocks])
    up_in = pltpu.make_async_copy(up_hbm.at[0], up_v, in_sem.at[blocks + 1])
    routes_in = pltpu.make_async_copy(routes_hbm, routes_v, in_sem.at[blocks + 2])
    gatew_in = pltpu.make_async_copy(gatew_hbm, gatew_v, in_sem.at[blocks + 3])
    routes_in.start()
    gatew_in.start()
    tok_in(0).start()
    gate_in.start()
    up_in.start()
    for b in range(1, blocks):
        tok_in(b).start()
    for b in range(blocks):
        for dy in range(ny):
            begin = pl.multiple_of(lax.rem(y + dy, ny) * hpart, hpart)
            pltpu.make_async_copy(
                weight_hbm.at[0, pl.ds(begin, hpart), b * COLS : (b + 1) * COLS],
                wts.at[b, dy * hpart : (dy + 1) * hpart],
                w_sem.at[b],
            ).start()

    earlier = (
        lax.broadcasted_iota(jnp.int32, (tokens, tokens), 0)
        < lax.broadcasted_iota(jnp.int32, (tokens, tokens), 1)
    )
    ahead[...] = jnp.where(earlier, 1.0, 0.0).astype(BF16)
    routes_in.wait()
    gatew_in.wait()
    meta[0, 0:topk, :] = routes_v[...].astype(F32)
    meta[0, topk : 2 * topk, :] = gatew_v[...].astype(F32)

    def ranks(s, ids):
        member = jnp.zeros(ids.shape, F32)
        gate_of = jnp.zeros(ids.shape, F32)
        for k in range(topk):
            hit = meta[s, k : k + 1, :] == ids
            member = jnp.where(hit, 1.0, member)
            gate_of = jnp.where(hit, meta[s, topk + k : topk + k + 1, :], gate_of)
        rank = jnp.dot(member.astype(BF16), ahead[...], preferred_element_type=F32)
        return jnp.where(member > 0.0, rank, -100.0), gate_of

    def rel_expert(r):
        i = r // nd
        half = (i + 1) // 2
        dz = jnp.where(i % 2 == 1, half, -half)
        d = r % nd
        return ((x + d // nc) % nx) * (nz * nc) + ((z + nz - dz) % nz) * nc + (c + d % nc) % nc

    def zmsg(buf, sem, b, step, up):
        src = 0 if step == 1 else (2 * (step - 1) if up else 2 * (step - 1) - 1)
        extent = buf.shape[1]
        if step < nz // 2:
            dst = 2 * step if up else 2 * step - 1
            key = dst
            part = slice(0, extent)
        else:
            dst = nz - 1
            key = dst if up else 0
            part = slice(0, extent // 2) if up else slice(extent // 2, extent)
        return send(
            buf.at[src, part], buf.at[dst, part], zsend.at[sem], zrecv.at[sem, key],
            device(0, 1 if up else -1, 0, 0),
        )

    def zblock(b, step, up):
        return zmsg(tok.at[b], b, b, step, up)

    def zmeta(step, up):
        return zmsg(meta, blocks, 0, step, up)

    def build_pick(which):
        lane = lax.broadcasted_iota(jnp.int32, (TILE, tokens), 0)
        d_id = lax.broadcasted_iota(jnp.int32, (nd, tokens), 0)
        ids = (((x + d_id // nc) % nx) * nz + z) * nc + (c + d_id % nc) % nc
        for s in which:
            rank_of, gate_of = ranks(s, ids.astype(F32))
            for d in range(nd):
                target = xmr.at[0] if d == 0 else xm.at[d]
                line = rank_of[d : d + 1, :]
                target[s : s + 1, :] = line
                target[nz + s : nz + s + 1, :] = gate_of[d : d + 1, :]
                span = slice(d * TILE, (d + 1) * TILE)
                pick[s, span, :] = jnp.where(line == lane.astype(F32), 1.0, 0.0).astype(BF16)
                more = jnp.where(lane // extra == s, TILE + lane % extra, -1).astype(F32)
                pick_more[span, s * tokens : (s + 1) * tokens] = jnp.where(
                    line == more, 1.0, 0.0
                ).astype(BF16)

    def back(d):
        return ((nx - d // nc) % nx) * nc + (nc - d % nc) % nc

    far_first = sorted(range(1, nd), key=lambda d: -min(d // nc, nx - d // nc))

    def xmeta(d):
        return send(
            xm.at[d], xmr.at[back(d)], xsend.at[blocks], xrecv.at[blocks],
            device(d // nc, 0, d % nc, 0),
        )

    def place(b, n, got):
        got = got.astype(BF16)
        rows[b, 0, n * TILE : (n + 1) * TILE, :] = got[0:TILE]
        for d in range(1, nd):
            xs[b, d, n * TILE : (n + 1) * TILE, :] = got[d * TILE : (d + 1) * TILE]

    def forward(b, first, last, sem):
        span = slice(first * TILE, (last + 1) * TILE)
        for d in far_first:
            send(
                xs.at[b, d, span], rows.at[b, back(d), span], xsend.at[sem], xrecv.at[sem],
                device(d // nc, 0, d % nc, 0),
            ).start()

    def select(b, which):
        for s in which:
            place(b, s, jnp.dot(pick[s], tok[b, s], preferred_element_type=F32))
        last = which[-1]
        if last == nz - 1:
            every = tok[b].reshape(nz * tokens, COLS)
            place(b, nz, jnp.dot(pick_more[...], every, preferred_element_type=F32))
            last = nz
        if last >= LATE:
            forward(b, which[0], last, b)
        else:
            pl.when(b < blocks - 1)(lambda: forward(b, which[0], last, b))

    pl.semaphore_wait(barrier, 2 + (nd - 1) + (ny - 1))
    for up in (True, False):
        zmeta(1, up).start()
    tok_in(0).wait()
    for up in (True, False):
        zblock(0, 1, up).start()
    build_pick((0,))
    select(0, (0,))
    for b in range(1, 3):
        tok_in(b).wait()
        if b == 1:
            for up in (True, False):
                zblock(1, 1, up).start()
        select(b, (0,))

    group = nz * nc * cap
    gate_in.wait()
    up_in.wait()
    row = lax.broadcasted_iota(jnp.int32, (group, group), 0)
    col = lax.broadcasted_iota(jnp.int32, (group, group), 1)
    dc = jnp.zeros_like(row)
    for n in range(1, nc):
        dc = jnp.where(row >= n * per, n, dc)
    inner = row - dc * per
    i = jnp.where(inner < nz * TILE, inner // TILE, (inner - nz * TILE) // extra)
    j = jnp.where(inner < nz * TILE, inner % TILE, TILE + inner % extra)
    half = (i + 1) // 2
    zs_of = (z + nz + jnp.where(i % 2 == 1, half, -half)) % nz
    cs_of = (c + dc) % nc
    perm = jnp.where((zs_of * nc + cs_of) * cap + j == col, 1.0, 0.0).astype(BF16)
    for dx in range(nx):
        begin = pl.multiple_of(lax.rem(x + dx, nx) * group, 16)
        gv = gate_v[pl.ds(begin, group), :].astype(F32)
        uv = up_v[pl.ds(begin, group), :].astype(F32)
        raw[...] = (gv / (1.0 + jnp.exp(-gv)) * uv).astype(BF16)
        hid[dx * group : (dx + 1) * group, 0:hpart] = jnp.dot(
            perm, raw[...], preferred_element_type=F32
        ).astype(BF16)

    def ypart(dy, first):
        return hid.at[
            0 : slots // 2 if first else slots, dy * hpart : (dy + 1) * hpart
        ] if first else hid.at[slots // 2 : slots, dy * hpart : (dy + 1) * hpart]

    def ymsg(n):
        up, first, src, dst = (
            (True, True, 0, 3), (False, False, 0, 1), (True, False, 0, 3),
            (False, True, 0, 1), (True, True, 3, 2), (False, False, 1, 2),
        )[n]
        return send(
            ypart(src, first), ypart(dst, first), ysend.at[n], yrecv.at[n],
            device(0, 0, 0, 1 if up else -1),
        )

    if ny > 1:
        for n in range(4):
            ymsg(n).start()
    eye = jnp.where(
        lax.broadcasted_iota(jnp.int32, (hpart, hpart), 0)
        == lax.broadcasted_iota(jnp.int32, (hpart, hpart), 1), 1.0, 0.0,
    ).astype(BF16)

    def turn(dy):
        hid_t[dy * hpart : (dy + 1) * hpart, :] = lax.dot_general(
            eye, hid[:, dy * hpart : (dy + 1) * hpart], (((1,), (1,)), ((), ())),
            preferred_element_type=F32,
        ).astype(BF16)

    turn(0)
    rel_ids = rel_expert(lax.broadcasted_iota(jnp.int32, (experts, tokens), 0)).astype(F32)
    rank_rel[...] = ranks(0, rel_ids)[0]
    for b in range(3, blocks):
        tok_in(b).wait()
    acc[...] = jnp.zeros_like(acc)
    sgp[...] = jnp.zeros_like(sgp)
    sgp_near[...] = jnp.zeros_like(sgp_near)
    zs[...] = jnp.zeros_like(zs)

    def all_of(buf, sem):
        pltpu.make_async_copy(buf, buf, sem).wait()

    def build_gates():
        sub = lax.broadcasted_iota(jnp.int32, (8, tokens), 0)

        def one(q, carry):
            for n in range(per // 8):
                value = jnp.zeros((8, tokens), F32)
                if n * 8 < nz * TILE:
                    wanted = [(n * 8 // TILE, sub + n * 8 % TILE)]
                else:
                    first = n * 8 - nz * TILE
                    wanted = [
                        (s, jnp.where((sub + first) // extra == s, TILE + (sub + first) % extra, -1))
                        for s in range(first // extra, (first + 7) // extra + 1)
                    ]
                for s, rank_at in wanted:
                    hit = xmr[q, s : s + 1, :] == rank_at.astype(F32)
                    value = jnp.where(hit, xmr[q, nz + s : nz + s + 1, :], value)
                total = jnp.sum(value, axis=1, keepdims=True)
                gates[pl.ds(pl.multiple_of(q * per + n * 8, 8), 8), :] = jnp.broadcast_to(
                    total, (8, tokens)
                )
            return carry

        lax.fori_loop(0, nd, one, 0)

    near = LATE * TILE

    def yback(part, dy):
        src, dst = ((sgp, sgy), (sgp_near, sgy_near))[part]
        return send(
            src, dst.at[(ny - dy) % ny], tsend.at[part], trecv.at[part], device(0, 0, 0, dy)
        )

    def xback(part, d):
        src, dst = ((sgt, sgx), (sgt_near, sgx_near))[part]
        return send(
            src.at[d], dst.at[back(d)], tsend.at[2 + part], trecv.at[2 + part],
            device(d // nc, 0, d % nc, 0),
        )

    def zback(i):
        sem = 4 if i >= LATE else 5
        return send(zs.at[i], zin.at[i], tsend.at[sem], trecv.at[sem], device(0, zdelta(i), 0, 0))

    def reduce_slots(part):
        ones = jnp.ones((8, tokens), F32)
        buf = (sgp, sgp_near)[part]
        lo, hi = ((near, per), (0, near))[part]
        for q in range(nd):
            line = lax.dot_general(
                ones, acc[q * per + lo : q * per + hi, :], (((1,), (1,)), ((), ())),
                preferred_element_type=F32, precision=lax.Precision.HIGHEST,
            )
            buf[q : q + 1, 0 : hi - lo] = line[0:1, :]
        for dy in range(1, ny):
            yback(part, dy).start()

    def sum_over_y(part):
        buf, got, out, arrived = ((sgp, sgy, sgt, sgx), (sgp_near, sgy_near, sgt_near, sgx_near))[part]
        total = buf[...]
        if ny > 1:
            all_of(got.at[1:ny], trecv.at[part])
            for dy in range(1, ny):
                total = total + got[dy]
        for d in far_first:
            out[d] = total[d : d + 1, :]
            xback(part, d).start()
        arrived[0] = total[0:1, :]

    def finish():
        sum_over_y(0)
        sum_over_y(1)
        all_of(sgx.at[1:nd], trecv.at[2])
        for d in range(nd):
            zrow[d : d + 1, :] = sgx[d]
        for s in range(nz - 1, LATE - 1, -1):
            zs[s, :, 0:TILE] = zrow[:, (s - LATE) * TILE : (s - LATE + 1) * TILE]
            more = (nz - LATE) * TILE + s * extra
            zs[s, :, TILE:cap] = zrow[:, more : more + extra]
            zback(s).start()
        all_of(sgx_near.at[1:nd], trecv.at[3])
        for d in range(nd):
            zrow_near[d : d + 1, :] = sgx_near[d]
        for s in range(LATE - 1, -1, -1):
            target = zs.at[s] if s else zin.at[0]
            target[:, 0:TILE] = zrow_near[:, s * TILE : (s + 1) * TILE]
            more = (nz - LATE) * TILE + s * extra
            target[:, TILE:cap] = zrow[:, more : more + extra]
            if s:
                zback(s).start()
        all_of(zin.at[LATE:nz], trecv.at[4])
        all_of(zin.at[1:LATE], trecv.at[5])
        values = zin[...].reshape(nz * nd, 128)
        rr = rank_rel[...]
        value = jnp.zeros((experts, tokens), F32)
        for n in range(cap):
            value = jnp.where(rr == float(n), values[:, n : n + 1], value)
        for k in range(topk):
            hit = meta[0, k : k + 1, :] == rel_ids
            dg_ref[k : k + 1, :] = jnp.sum(jnp.where(hit, value, 0.0), axis=0, keepdims=True)

    def consume(b):
        all_of(wts.at[b], w_sem.at[b])
        eo[...] = jnp.dot(hid[...], wts[b], preferred_element_type=F32)

        def meet(lo, hi):
            def one(q, carry):
                span = pl.ds(pl.multiple_of(q * per + lo, TILE), hi - lo)
                r = rows[b, q, lo:hi, :].astype(F32)
                prod = r * eo[span, :]
                acc[span, :] += prod[:, 0:128] + prod[:, 128:256]
                gv = gates[span, :]
                scaled[span, 0:128] = (r[:, 0:128] * gv).astype(BF16)
                scaled[span, 128:256] = (r[:, 128:256] * gv).astype(BF16)
                return carry

            lax.fori_loop(0, nd, one, 0)

        @pl.when(b < blocks - 1)
        def _():
            all_of(rows.at[b, 1:nd], xrecv.at[b])
            meet(0, per)

        @pl.when(b == blocks - 1)
        def _():
            all_of(rows.at[blocks - 1, 1:nd, near:per], xrecv.at[blocks - 1])
            meet(near, per)
            reduce_slots(0)
            all_of(rows.at[blocks - 1, 1:nd, 0:near], xrecv.at[blocks + 1])
            meet(0, near)
            reduce_slots(1)

        span = pl.ds(pl.multiple_of(b * COLS, COLS), COLS)
        for dy in range(ny):
            begin = pl.multiple_of(lax.rem(y + dy, ny) * hpart, hpart)
            dw_ref[pl.ds(begin, hpart), span] = jnp.dot(
                hid_t[dy * hpart : (dy + 1) * hpart, :], scaled[...], preferred_element_type=F32
            ).astype(BF16)

    depth = nz // 2

    def slot(t, carry):
        for step in range(depth, 0, -1):
            b = t - step

            def act(step=step, b=b):
                @pl.when(b == 0)
                def _():
                    for up in (True, False):
                        zmeta(step, up).wait_recv()
                        if step < depth:
                            zmeta(step + 1, up).start()

                for up in (True, False):
                    zblock(b, step, up).wait_recv()
                    if step < depth:
                        zblock(b, step + 1, up).start()

                fresh = (2 * step - 1, 2 * step) if step < depth else (nz - 1,)

                @pl.when(b == 0)
                def _():
                    build_pick(fresh)
                    if step == depth:
                        for d in far_first:
                            xmeta(d).start()

                select(b, fresh)
                if step == depth:
                    @pl.when(b == blocks - 1)
                    def _():
                        select(b, (0,))
                        forward(b, 0, LATE - 1, blocks + 1)

            pl.when((b >= 0) & (b < blocks))(act)


        @pl.when(t + 1 < blocks)
        def _():
            for up in (True, False):
                zblock(t + 1, 1, up).start()

        for own in (2 * t + 1, 2 * t + 2):
            @pl.when(own < blocks - 1)
            def _(own=own):
                select(own, (0,))

        if ny > 1:
            @pl.when(t == depth)
            def _():
                for n in (0, 1):
                    ymsg(n).wait_recv()
                for n in (4, 5):
                    ymsg(n).start()

        @pl.when(t == depth + LAG)
        def _():
            all_of(xmr.at[1:nd], xrecv.at[blocks])
            build_gates()
            if ny > 1:
                for n in range(2, 6):
                    ymsg(n).wait_recv()
                for dy in range(1, ny):
                    turn(dy)

        b = t - depth - LAG

        @pl.when(b >= 0)
        def _():
            consume(b)

        return carry

    lax.fori_loop(1, blocks + depth + LAG, slot, 0)
    finish()

    for b in range(blocks):
        all_of(tok.at[b, 1:nz], zsend.at[b])
    for b in range(blocks - 1):
        all_of(xs.at[b, 1:nd], xsend.at[b])
    all_of(xs.at[blocks - 1, 1:nd, near:per], xsend.at[blocks - 1])
    all_of(xs.at[blocks - 1, 1:nd, 0:near], xsend.at[blocks + 1])
    all_of(meta.at[1:nz], zsend.at[blocks])
    all_of(xm.at[1:nd], xsend.at[blocks])
    if ny > 1:
        for n in range(6):
            ymsg(n).wait_send()
        all_of(sgy.at[1:ny], tsend.at[0])
        all_of(sgy_near.at[1:ny], tsend.at[1])
    all_of(sgx.at[1:nd], tsend.at[2])
    all_of(sgx_near.at[1:nd], tsend.at[3])
    all_of(zs.at[LATE:nz], tsend.at[4])
    all_of(zs.at[1:LATE], tsend.at[5])


def local(sizes, out_grad, gate_weights, routes, gate_pre, up_pre, down_weight):
    nx, nz, nc, ny = sizes
    routes, gate_weights = routes.T, gate_weights.T
    topk, tokens = routes.shape
    width = out_grad.shape[1]
    blocks = width // COLS
    experts = nx * nz * nc
    nd = nx * nc
    slots, hpart = gate_pre.shape[1:]
    hidden = down_weight.shape[1]
    cap = slots // experts
    per = nz * cap
    hbm = pl.BlockSpec(memory_space=pltpu.HBM)
    vmem = pl.BlockSpec(memory_space=pltpu.VMEM)
    dma = pltpu.SemaphoreType.DMA
    dw, dg = pl.pallas_call(
        functools.partial(kernel, nx, nz, nc, ny, cap),
        out_shape=(
            jax.ShapeDtypeStruct((hidden, width), BF16),
            jax.ShapeDtypeStruct((topk, tokens), F32),
        ),
        in_specs=[hbm] * 6,
        out_specs=(vmem, vmem),
        scratch_shapes=[
            pltpu.VMEM((topk, tokens), jnp.int32),
            pltpu.VMEM((topk, tokens), BF16),
            pltpu.VMEM((blocks, nz, tokens, COLS), BF16),
            pltpu.VMEM((nz, 2 * topk, tokens), F32),
            pltpu.VMEM((tokens, tokens), BF16),
            pltpu.VMEM((nz, nd * TILE, tokens), BF16),
            pltpu.VMEM((nd * TILE, nz * tokens), BF16),
            pltpu.VMEM((blocks, nd, per, COLS), BF16),
            pltpu.VMEM((nd, 2 * nz, tokens), F32),
            pltpu.VMEM((blocks, nd, per, COLS), BF16),
            pltpu.VMEM((nd, 2 * nz, tokens), F32),
            pltpu.VMEM((slots, hpart), BF16),
            pltpu.VMEM((slots, hpart), BF16),
            pltpu.VMEM((nz * nc * cap, hpart), BF16),
            pltpu.VMEM((slots, hidden), BF16),
            pltpu.VMEM((hidden, slots), BF16),
            pltpu.VMEM((blocks, hidden, COLS), BF16),
            pltpu.VMEM((slots, COLS), F32),
            pltpu.VMEM((slots, 128), F32),
            pltpu.VMEM((slots, 128), F32),
            pltpu.VMEM((slots, COLS), BF16),
            pltpu.VMEM((experts, tokens), F32),
            pltpu.VMEM((nd, 128), F32),
            pltpu.VMEM((ny, nd, 128), F32),
            pltpu.VMEM((nd, 1, 128), F32),
            pltpu.VMEM((nd, 1, 128), F32),
            pltpu.VMEM((nd, 128), F32),
            pltpu.VMEM((nd, 128), F32),
            pltpu.VMEM((ny, nd, 128), F32),
            pltpu.VMEM((nd, 1, 128), F32),
            pltpu.VMEM((nd, 1, 128), F32),
            pltpu.VMEM((nd, 128), F32),
            pltpu.VMEM((nz, nd, 128), F32),
            pltpu.VMEM((nz, nd, 128), F32),
            dma((blocks + 4,)),
            dma((blocks,)),
            dma((blocks + 1,)),
            dma((blocks + 1, nz)),
            dma((blocks + 2,)),
            dma((blocks + 2,)),
            dma((6,)),
            dma((6,)),
            dma((6,)),
            dma((6,)),
        ],
        compiler_params=pltpu.CompilerParams(collective_id=0, has_side_effects=True, vmem_limit_bytes=44 * 2**20),
    )(
        *(
            pltpu.with_memory_space_constraint(v, pltpu.HBM)
            for v in (routes, gate_weights, out_grad, gate_pre, up_pre, down_weight)
        )
    )
    return dw[None], dg.T


def solution(mesh):
    ny = mesh.shape["et"]
    nx = mesh.shape["ep"] // (NZ * NC)
    in_specs = (
        P("ep", "et"),
        P("ep", None),
        P("ep", None),
        P("ep", None, "et"),
        P("ep", None, "et"),
        P("ep", None, "et"),
    )
    out_specs = (P("ep", None, "et"), P("ep", None))
    return jax.shard_map(
        functools.partial(local, (nx, NZ, NC, ny)),
        mesh=mesh, in_specs=in_specs, out_specs=out_specs, check_vma=False,
    )
```

```python
import functools

import jax
import jax.numpy as jnp
from jax import lax
from jax.experimental import pallas as pl
from jax.experimental.pallas import tpu as pltpu
from jax.sharding import PartitionSpec as P

MESH = pl.DeviceIdType.MESH
F32 = jnp.float32
BF16 = jnp.bfloat16
NZ = 8
NC = 2
COLS = 256
LAG = 2
LATE = 3
TILE = 16


def zdelta(i):
    half = (i + 1) // 2
    return half if i % 2 else -half


def kernel(
    nx, nz, nc, ny, cap,
    routes_hbm, gatew_hbm, grad_hbm, gate_hbm, up_hbm, weight_hbm,
    dw_ref, dg_ref,
    routes_v, gatew_v, tok, meta, ahead, pick, pick_more, xs, xm, rows, xmr, gate_v, up_v, raw, hid, hid_t, wts, eo, gates, acc,
    scaled, rank_rel, sgp, sgy, sgt, sgx, zrow, sgp_near, sgy_near, sgt_near, sgx_near, zrow_near, zs, zin,
    in_sem, w_sem, zsend, zrecv, xsend, xrecv, ysend, yrecv, tsend, trecv,
):
    nd = nx * nc
    experts = nx * nz * nc
    topk, tokens = routes_hbm.shape
    extra = cap - TILE
    blocks = tok.shape[0]
    per = nz * cap
    slots = nd * per
    hpart = gate_v.shape[1]
    ep, y = lax.axis_index("ep"), lax.axis_index("et")
    x, z, c = ep // (nz * nc), (ep // nc) % nz, ep % nc

    def device(dx, dz, dc, dy):
        xx, zz = lax.rem(x + (dx + nx), nx), lax.rem(z + (dz + nz), nz)
        cc, yy = lax.rem(c + dc, nc), lax.rem(y + (dy + ny), ny)
        return ((xx * nz + zz) * nc + cc, yy)

    def send(src, dst, ssem, rsem, to):
        return pltpu.make_async_remote_copy(
            src_ref=src, dst_ref=dst, send_sem=ssem, recv_sem=rsem, device_id=to, device_id_type=MESH
        )

    def tok_in(b):
        return pltpu.make_async_copy(
            grad_hbm.at[:, pl.ds(pl.multiple_of(b * COLS, COLS), COLS)], tok.at[b, 0], in_sem.at[b]
        )

    gate_in = pltpu.make_async_copy(gate_hbm.at[0], gate_v, in_sem.at[blocks])
    up_in = pltpu.make_async_copy(up_hbm.at[0], up_v, in_sem.at[blocks + 1])
    routes_in = pltpu.make_async_copy(routes_hbm, routes_v, in_sem.at[blocks + 2])
    gatew_in = pltpu.make_async_copy(gatew_hbm, gatew_v, in_sem.at[blocks + 3])
    routes_in.start()
    gatew_in.start()
    tok_in(0).start()

    plane = [(d // nc, d % nc) for d in range(1, nd)]
    barrier = pltpu.get_barrier_semaphore()
    for dz in (1, nz - 1):
        pl.semaphore_signal(barrier, inc=1, device_id=device(0, dz, 0, 0), device_id_type=MESH)
    for dx, dc in plane:
        pl.semaphore_signal(barrier, inc=1, device_id=device(dx, 0, dc, 0), device_id_type=MESH)
    for dy in range(1, ny):
        pl.semaphore_signal(barrier, inc=1, device_id=device(0, 0, 0, dy), device_id_type=MESH)
    tok_in(1).start()
    tok_in(2).start()
    gate_in.start()
    up_in.start()

    earlier = (
        lax.broadcasted_iota(jnp.int32, (tokens, tokens), 0)
        < lax.broadcasted_iota(jnp.int32, (tokens, tokens), 1)
    )
    ahead[...] = jnp.where(earlier, 1.0, 0.0).astype(BF16)
    routes_in.wait()
    gatew_in.wait()
    meta[0, 0:topk, :] = routes_v[...].astype(F32)
    meta[0, topk : 2 * topk, :] = gatew_v[...].astype(F32)

    def ranks(s, ids):
        member = jnp.zeros(ids.shape, F32)
        gate_of = jnp.zeros(ids.shape, F32)
        for k in range(topk):
            hit = meta[s, k : k + 1, :] == ids
            member = jnp.where(hit, 1.0, member)
            gate_of = jnp.where(hit, meta[s, topk + k : topk + k + 1, :], gate_of)
        rank = jnp.dot(member.astype(BF16), ahead[...], preferred_element_type=F32)
        return jnp.where(member > 0.0, rank, -100.0), gate_of

    def rel_expert(r):
        i = r // nd
        half = (i + 1) // 2
        dz = jnp.where(i % 2 == 1, half, -half)
        d = r % nd
        return ((x + d // nc) % nx) * (nz * nc) + ((z + nz - dz) % nz) * nc + (c + d % nc) % nc

    def zmsg(buf, sem, b, step, up):
        src = 0 if step == 1 else (2 * (step - 1) if up else 2 * (step - 1) - 1)
        extent = buf.shape[1]
        if step < nz // 2:
            dst = 2 * step if up else 2 * step - 1
            key = dst
            part = slice(0, extent)
        else:
            dst = nz - 1
            key = dst if up else 0
            part = slice(0, extent // 2) if up else slice(extent // 2, extent)
        return send(
            buf.at[src, part], buf.at[dst, part], zsend.at[sem], zrecv.at[sem, key],
            device(0, 1 if up else -1, 0, 0),
        )

    def zblock(b, step, up):
        return zmsg(tok.at[b], b, b, step, up)

    def zmeta(step, up):
        return zmsg(meta, blocks, 0, step, up)

    def build_pick(which):
        lane = lax.broadcasted_iota(jnp.int32, (TILE, tokens), 0)
        d_id = lax.broadcasted_iota(jnp.int32, (nd, tokens), 0)
        ids = (((x + d_id // nc) % nx) * nz + z) * nc + (c + d_id % nc) % nc
        for s in which:
            rank_of, gate_of = ranks(s, ids.astype(F32))
            for d in range(nd):
                target = xmr.at[0] if d == 0 else xm.at[d]
                line = rank_of[d : d + 1, :]
                target[s : s + 1, :] = line
                target[nz + s : nz + s + 1, :] = gate_of[d : d + 1, :]
                span = slice(d * TILE, (d + 1) * TILE)
                pick[s, span, :] = jnp.where(line == lane.astype(F32), 1.0, 0.0).astype(BF16)
                more = jnp.where(lane // extra == s, TILE + lane % extra, -1).astype(F32)
                pick_more[span, s * tokens : (s + 1) * tokens] = jnp.where(
                    line == more, 1.0, 0.0
                ).astype(BF16)

    def back(d):
        return ((nx - d // nc) % nx) * nc + (nc - d % nc) % nc

    far_first = sorted(range(1, nd), key=lambda d: -min(d // nc, nx - d // nc))

    def xmeta(d):
        return send(
            xm.at[d], xmr.at[back(d)], xsend.at[blocks], xrecv.at[blocks],
            device(d // nc, 0, d % nc, 0),
        )

    def place(b, n, got):
        got = got.astype(BF16)
        rows[b, 0, n * TILE : (n + 1) * TILE, :] = got[0:TILE]
        for d in range(1, nd):
            xs[b, d, n * TILE : (n + 1) * TILE, :] = got[d * TILE : (d + 1) * TILE]

    def forward(b, first, last, sem):
        span = slice(first * TILE, (last + 1) * TILE)
        for d in far_first:
            send(
                xs.at[b, d, span], rows.at[b, back(d), span], xsend.at[sem], xrecv.at[sem],
                device(d // nc, 0, d % nc, 0),
            ).start()

    def select(b, which):
        for s in which:
            place(b, s, jnp.dot(pick[s], tok[b, s], preferred_element_type=F32))
        last = which[-1]
        if last == nz - 1:
            every = tok[b].reshape(nz * tokens, COLS)
            place(b, nz, jnp.dot(pick_more[...], every, preferred_element_type=F32))
            last = nz
        if last >= LATE:
            forward(b, which[0], last, b)
        else:
            pl.when(b < blocks - 1)(lambda: forward(b, which[0], last, b))

    pl.semaphore_wait(barrier, 2 + (nd - 1) + (ny - 1))
    for up in (True, False):
        zmeta(1, up).start()
    tok_in(0).wait()
    for up in (True, False):
        zblock(0, 1, up).start()
    build_pick((0,))
    select(0, (0,))
    for b in range(1, 3):
        tok_in(b).wait()
        if b == 1:
            for up in (True, False):
                zblock(1, 1, up).start()
        select(b, (0,))

    for b in range(3, blocks):
        tok_in(b).start()
    for b in range(blocks):
        for dy in range(ny):
            begin = pl.multiple_of(lax.rem(y + dy, ny) * hpart, hpart)
            pltpu.make_async_copy(
                weight_hbm.at[0, pl.ds(begin, hpart), b * COLS : (b + 1) * COLS],
                wts.at[b, dy * hpart : (dy + 1) * hpart],
                w_sem.at[b],
            ).start()

    group = nz * nc * cap
    gate_in.wait()
    up_in.wait()
    row = lax.broadcasted_iota(jnp.int32, (group, group), 0)
    col = lax.broadcasted_iota(jnp.int32, (group, group), 1)
    dc = jnp.zeros_like(row)
    for n in range(1, nc):
        dc = jnp.where(row >= n * per, n, dc)
    inner = row - dc * per
    i = jnp.where(inner < nz * TILE, inner // TILE, (inner - nz * TILE) // extra)
    j = jnp.where(inner < nz * TILE, inner % TILE, TILE + inner % extra)
    half = (i + 1) // 2
    zs_of = (z + nz + jnp.where(i % 2 == 1, half, -half)) % nz
    cs_of = (c + dc) % nc
    perm = jnp.where((zs_of * nc + cs_of) * cap + j == col, 1.0, 0.0).astype(BF16)
    for dx in range(nx):
        begin = pl.multiple_of(lax.rem(x + dx, nx) * group, 16)
        gv = gate_v[pl.ds(begin, group), :].astype(F32)
        uv = up_v[pl.ds(begin, group), :].astype(F32)
        raw[...] = (gv / (1.0 + jnp.exp(-gv)) * uv).astype(BF16)
        hid[dx * group : (dx + 1) * group, 0:hpart] = jnp.dot(
            perm, raw[...], preferred_element_type=F32
        ).astype(BF16)

    def ypart(dy, first):
        return hid.at[
            0 : slots // 2 if first else slots, dy * hpart : (dy + 1) * hpart
        ] if first else hid.at[slots // 2 : slots, dy * hpart : (dy + 1) * hpart]

    def ymsg(n):
        up, first, src, dst = (
            (True, True, 0, 3), (False, False, 0, 1), (True, False, 0, 3),
            (False, True, 0, 1), (True, True, 3, 2), (False, False, 1, 2),
        )[n]
        return send(
            ypart(src, first), ypart(dst, first), ysend.at[n], yrecv.at[n],
            device(0, 0, 0, 1 if up else -1),
        )

    if ny > 1:
        for n in range(4):
            ymsg(n).start()
    eye = jnp.where(
        lax.broadcasted_iota(jnp.int32, (hpart, hpart), 0)
        == lax.broadcasted_iota(jnp.int32, (hpart, hpart), 1), 1.0, 0.0,
    ).astype(BF16)

    def turn(dy):
        hid_t[dy * hpart : (dy + 1) * hpart, :] = lax.dot_general(
            eye, hid[:, dy * hpart : (dy + 1) * hpart], (((1,), (1,)), ((), ())),
            preferred_element_type=F32,
        ).astype(BF16)

    turn(0)
    rel_ids = rel_expert(lax.broadcasted_iota(jnp.int32, (experts, tokens), 0)).astype(F32)
    rank_rel[...] = ranks(0, rel_ids)[0]
    for b in range(3, blocks):
        tok_in(b).wait()
    acc[...] = jnp.zeros_like(acc)
    sgp[...] = jnp.zeros_like(sgp)
    sgp_near[...] = jnp.zeros_like(sgp_near)
    zs[...] = jnp.zeros_like(zs)

    def all_of(buf, sem):
        pltpu.make_async_copy(buf, buf, sem).wait()

    def build_gates():
        sub = lax.broadcasted_iota(jnp.int32, (8, tokens), 0)

        def one(q, carry):
            for n in range(per // 8):
                value = jnp.zeros((8, tokens), F32)
                if n * 8 < nz * TILE:
                    wanted = [(n * 8 // TILE, sub + n * 8 % TILE)]
                else:
                    first = n * 8 - nz * TILE
                    wanted = [
                        (s, jnp.where((sub + first) // extra == s, TILE + (sub + first) % extra, -1))
                        for s in range(first // extra, (first + 7) // extra + 1)
                    ]
                for s, rank_at in wanted:
                    hit = xmr[q, s : s + 1, :] == rank_at.astype(F32)
                    value = jnp.where(hit, xmr[q, nz + s : nz + s + 1, :], value)
                total = jnp.sum(value, axis=1, keepdims=True)
                gates[pl.ds(pl.multiple_of(q * per + n * 8, 8), 8), :] = jnp.broadcast_to(
                    total, (8, tokens)
                )
            return carry

        lax.fori_loop(0, nd, one, 0)

    def weight_grad(b):
        span = pl.ds(b * COLS if isinstance(b, int) else pl.multiple_of(b * COLS, COLS), COLS)
        for dy in range(ny):
            begin = pl.multiple_of(lax.rem(y + dy, ny) * hpart, hpart)
            dw_ref[pl.ds(begin, hpart), span] = jnp.dot(
                hid_t[dy * hpart : (dy + 1) * hpart, :], scaled[...], preferred_element_type=F32
            ).astype(BF16)

    near = LATE * TILE

    def yback(part, dy):
        src, dst = ((sgp, sgy), (sgp_near, sgy_near))[part]
        return send(
            src, dst.at[(ny - dy) % ny], tsend.at[part], trecv.at[part], device(0, 0, 0, dy)
        )

    def xback(part, d):
        src, dst = ((sgt, sgx), (sgt_near, sgx_near))[part]
        return send(
            src.at[d], dst.at[back(d)], tsend.at[2 + part], trecv.at[2 + part],
            device(d // nc, 0, d % nc, 0),
        )

    def zback(i):
        sem = 4 if i >= LATE else 5
        return send(zs.at[i], zin.at[i], tsend.at[sem], trecv.at[sem], device(0, zdelta(i), 0, 0))

    def reduce_slots(part):
        ones = jnp.ones((8, tokens), F32)
        buf = (sgp, sgp_near)[part]
        lo, hi = ((near, per), (0, near))[part]
        for q in range(nd):
            line = lax.dot_general(
                ones, acc[q * per + lo : q * per + hi, :], (((1,), (1,)), ((), ())),
                preferred_element_type=F32, precision=lax.Precision.HIGHEST,
            )
            buf[q : q + 1, 0 : hi - lo] = line[0:1, :]
        for dy in sorted(range(1, ny), key=lambda dy: -min(dy, ny - dy)):
            yback(part, dy).start()

    def sum_over_y(part):
        buf, got, out, arrived = ((sgp, sgy, sgt, sgx), (sgp_near, sgy_near, sgt_near, sgx_near))[part]
        total = buf[...]
        if ny > 1:
            all_of(got.at[1:ny], trecv.at[part])
            for dy in range(1, ny):
                total = total + got[dy]
        for d in far_first:
            out[d] = total[d : d + 1, :]
            xback(part, d).start()
        arrived[0] = total[0:1, :]

    def finish():
        sum_over_y(0)
        sum_over_y(1)
        all_of(sgx.at[1:nd], trecv.at[2])
        for d in range(nd):
            zrow[d : d + 1, :] = sgx[d]
        for s in range(nz - 1, LATE - 1, -1):
            zs[s, :, 0:TILE] = zrow[:, (s - LATE) * TILE : (s - LATE + 1) * TILE]
            more = (nz - LATE) * TILE + s * extra
            zs[s, :, TILE:cap] = zrow[:, more : more + extra]
            zback(s).start()
        weight_grad(blocks - 1)
        all_of(sgx_near.at[1:nd], trecv.at[3])
        for d in range(nd):
            zrow_near[d : d + 1, :] = sgx_near[d]
        for s in range(LATE - 1, -1, -1):
            target = zs.at[s] if s else zin.at[0]
            target[:, 0:TILE] = zrow_near[:, s * TILE : (s + 1) * TILE]
            more = (nz - LATE) * TILE + s * extra
            target[:, TILE:cap] = zrow[:, more : more + extra]
            if s:
                zback(s).start()
        all_of(zin.at[LATE:nz], trecv.at[4])
        all_of(zin.at[1:LATE], trecv.at[5])
        values = zin[...].reshape(nz * nd, 128)
        rr = rank_rel[...]
        value = jnp.zeros((experts, tokens), F32)
        for n in range(cap):
            value = jnp.where(rr == float(n), values[:, n : n + 1], value)
        for k in range(topk):
            hit = meta[0, k : k + 1, :] == rel_ids
            dg_ref[k : k + 1, :] = jnp.sum(jnp.where(hit, value, 0.0), axis=0, keepdims=True)

    def consume(b):
        all_of(wts.at[b], w_sem.at[b])
        eo[...] = jnp.dot(hid[...], wts[b], preferred_element_type=F32)

        def meet(lo, hi):
            def one(q, carry):
                span = pl.ds(pl.multiple_of(q * per + lo, TILE), hi - lo)
                r = rows[b, q, lo:hi, :].astype(F32)
                prod = r * eo[span, :]
                acc[span, :] += prod[:, 0:128] + prod[:, 128:256]
                gv = gates[span, :]
                scaled[span, 0:128] = (r[:, 0:128] * gv).astype(BF16)
                scaled[span, 128:256] = (r[:, 128:256] * gv).astype(BF16)
                return carry

            lax.fori_loop(0, nd, one, 0)

        @pl.when(b < blocks - 1)
        def _():
            all_of(rows.at[b, 1:nd], xrecv.at[b])
            meet(0, per)

        @pl.when(b == blocks - 1)
        def _():
            all_of(rows.at[blocks - 1, 1:nd, near:per], xrecv.at[blocks - 1])
            meet(near, per)
            reduce_slots(0)
            all_of(rows.at[blocks - 1, 1:nd, 0:near], xrecv.at[blocks + 1])
            meet(0, near)
            reduce_slots(1)

        pl.when(b < blocks - 1)(lambda: weight_grad(b))

    depth = nz // 2

    def slot(t, carry):
        for step in range(depth, 0, -1):
            b = t - step

            def act(step=step, b=b):
                @pl.when(b == 0)
                def _():
                    for up in (True, False):
                        zmeta(step, up).wait_recv()
                        if step < depth:
                            zmeta(step + 1, up).start()

                for up in (True, False):
                    zblock(b, step, up).wait_recv()
                    if step < depth:
                        zblock(b, step + 1, up).start()

                fresh = (2 * step - 1, 2 * step) if step < depth else (nz - 1,)

                @pl.when(b == 0)
                def _():
                    build_pick(fresh)
                    if step == depth:
                        for d in far_first:
                            xmeta(d).start()

                select(b, fresh)
                if step == depth:
                    @pl.when(b == blocks - 1)
                    def _():
                        select(b, (0,))
                        forward(b, 0, LATE - 1, blocks + 1)

            pl.when((b >= 0) & (b < blocks))(act)


        @pl.when(t + 1 < blocks)
        def _():
            for up in (True, False):
                zblock(t + 1, 1, up).start()

        for own in (2 * t + 1, 2 * t + 2):
            @pl.when(own < blocks - 1)
            def _(own=own):
                select(own, (0,))

        if ny > 1:
            @pl.when(t == depth)
            def _():
                for n in (0, 1):
                    ymsg(n).wait_recv()
                for n in (4, 5):
                    ymsg(n).start()

        @pl.when(t == depth + LAG)
        def _():
            all_of(xmr.at[1:nd], xrecv.at[blocks])
            build_gates()
            if ny > 1:
                for n in range(2, 6):
                    ymsg(n).wait_recv()
                for dy in range(1, ny):
                    turn(dy)

        b = t - depth - LAG

        @pl.when(b >= 0)
        def _():
            consume(b)

        return carry

    lax.fori_loop(1, blocks + depth + LAG, slot, 0)
    finish()

    for b in range(blocks):
        all_of(tok.at[b, 1:nz], zsend.at[b])
    for b in range(blocks - 1):
        all_of(xs.at[b, 1:nd], xsend.at[b])
    all_of(xs.at[blocks - 1, 1:nd, near:per], xsend.at[blocks - 1])
    all_of(xs.at[blocks - 1, 1:nd, 0:near], xsend.at[blocks + 1])
    all_of(meta.at[1:nz], zsend.at[blocks])
    all_of(xm.at[1:nd], xsend.at[blocks])
    if ny > 1:
        for n in range(6):
            ymsg(n).wait_send()
        all_of(sgy.at[1:ny], tsend.at[0])
        all_of(sgy_near.at[1:ny], tsend.at[1])
    all_of(sgx.at[1:nd], tsend.at[2])
    all_of(sgx_near.at[1:nd], tsend.at[3])
    all_of(zs.at[LATE:nz], tsend.at[4])
    all_of(zs.at[1:LATE], tsend.at[5])


def local(sizes, out_grad, gate_weights, routes, gate_pre, up_pre, down_weight):
    nx, nz, nc, ny = sizes
    routes, gate_weights = routes.T, gate_weights.T
    topk, tokens = routes.shape
    width = out_grad.shape[1]
    blocks = width // COLS
    experts = nx * nz * nc
    nd = nx * nc
    slots, hpart = gate_pre.shape[1:]
    hidden = down_weight.shape[1]
    cap = slots // experts
    per = nz * cap
    hbm = pl.BlockSpec(memory_space=pltpu.HBM)
    vmem = pl.BlockSpec(memory_space=pltpu.VMEM)
    dma = pltpu.SemaphoreType.DMA
    dw, dg = pl.pallas_call(
        functools.partial(kernel, nx, nz, nc, ny, cap),
        out_shape=(
            jax.ShapeDtypeStruct((hidden, width), BF16),
            jax.ShapeDtypeStruct((topk, tokens), F32),
        ),
        in_specs=[hbm] * 6,
        out_specs=(vmem, vmem),
        scratch_shapes=[
            pltpu.VMEM((topk, tokens), jnp.int32),
            pltpu.VMEM((topk, tokens), BF16),
            pltpu.VMEM((blocks, nz, tokens, COLS), BF16),
            pltpu.VMEM((nz, 2 * topk, tokens), F32),
            pltpu.VMEM((tokens, tokens), BF16),
            pltpu.VMEM((nz, nd * TILE, tokens), BF16),
            pltpu.VMEM((nd * TILE, nz * tokens), BF16),
            pltpu.VMEM((blocks, nd, per, COLS), BF16),
            pltpu.VMEM((nd, 2 * nz, tokens), F32),
            pltpu.VMEM((blocks, nd, per, COLS), BF16),
            pltpu.VMEM((nd, 2 * nz, tokens), F32),
            pltpu.VMEM((slots, hpart), BF16),
            pltpu.VMEM((slots, hpart), BF16),
            pltpu.VMEM((nz * nc * cap, hpart), BF16),
            pltpu.VMEM((slots, hidden), BF16),
            pltpu.VMEM((hidden, slots), BF16),
            pltpu.VMEM((blocks, hidden, COLS), BF16),
            pltpu.VMEM((slots, COLS), F32),
            pltpu.VMEM((slots, 128), F32),
            pltpu.VMEM((slots, 128), F32),
            pltpu.VMEM((slots, COLS), BF16),
            pltpu.VMEM((experts, tokens), F32),
            pltpu.VMEM((nd, 128), F32),
            pltpu.VMEM((ny, nd, 128), F32),
            pltpu.VMEM((nd, 1, 128), F32),
            pltpu.VMEM((nd, 1, 128), F32),
            pltpu.VMEM((nd, 128), F32),
            pltpu.VMEM((nd, 128), F32),
            pltpu.VMEM((ny, nd, 128), F32),
            pltpu.VMEM((nd, 1, 128), F32),
            pltpu.VMEM((nd, 1, 128), F32),
            pltpu.VMEM((nd, 128), F32),
            pltpu.VMEM((nz, nd, 128), F32),
            pltpu.VMEM((nz, nd, 128), F32),
            dma((blocks + 4,)),
            dma((blocks,)),
            dma((blocks + 1,)),
            dma((blocks + 1, nz)),
            dma((blocks + 2,)),
            dma((blocks + 2,)),
            dma((6,)),
            dma((6,)),
            dma((6,)),
            dma((6,)),
        ],
        compiler_params=pltpu.CompilerParams(collective_id=0, has_side_effects=True, vmem_limit_bytes=44 * 2**20),
    )(
        *(
            pltpu.with_memory_space_constraint(v, pltpu.HBM)
            for v in (routes, gate_weights, out_grad, gate_pre, up_pre, down_weight)
        )
    )
    return dw[None], dg.T


def solution(mesh):
    ny = mesh.shape["et"]
    nx = mesh.shape["ep"] // (NZ * NC)
    in_specs = (
        P("ep", "et"),
        P("ep", None),
        P("ep", None),
        P("ep", None, "et"),
        P("ep", None, "et"),
        P("ep", None, "et"),
    )
    out_specs = (P("ep", None, "et"), P("ep", None))
    return jax.shard_map(
        functools.partial(local, (nx, NZ, NC, ny)),
        mesh=mesh, in_specs=in_specs, out_specs=out_specs, check_vma=False,
    )
```
